32 devices in a mesh: ctx: 8 (over z, x), tp: 4 (over y, core).
Axes of the slice: x: 2, y: 2, z: 4, core: 2. Of those that a mesh axis runs over, the one named last changes fastest.
Arguments:
- hidden: bfloat16 [1024, 3584], P('ctx', 'tp'), may hold values from -6 to 6
- norm_gain: float32 [3584], replicated, may hold values from 0.1 to 1.9
- w_query: bfloat16 [3584, 3584], P(None, 'tp'), may hold values from -0.09375 to 0.09375
- bias_query: float32 [3584], P('tp'), may hold values from -3 to 3
- w_key: bfloat16 [3584, 512], P(None, 'tp'), may hold values from -0.09375 to 0.09375
- bias_key: float32 [512], P('tp'), may hold values from -3 to 3
- w_value: bfloat16 [3584, 512], P(None, 'tp'), may hold values from -0.09375 to 0.09375
- bias_value: float32 [512], P('tp'), may hold values from -3 to 3
- cache_key: bfloat16 [2048, 512], P('ctx', 'tp'), may hold values from -64 to 64
- cache_value: bfloat16 [2048, 512], P('ctx', 'tp'), may hold values from -6 to 6
- keep: int32 [1024], replicated, may hold values from 0 to 1, as said below
- positions: int32 [3, 1024], replicated, may hold values from 0 to 2047
Outputs:
- attended: bfloat16 [1024, 3584], P('ctx', 'tp')
The draws below stay inside these ranges and needn't reach their ends.
Inputs may be any that keep to these rules, and one draw needn't show every extreme that they name: `keep`: exactly 512 tokens are kept; the counts kept by the 128-token blocks differ widely, and some block keeps all of its tokens.
All inputs are finite; a program needn't handle non-finite values.
Results may differ from the reference program's by a relative error of at most 0.0075.
The reference program's roundings to bfloat16 on the way count: a program that leaves them out, or rounds other values in their place, can miss the bound.
Values may be sent and summed in bfloat16 or wider, within the bound.
No kernel may reach another device: no remote copies, remote signals or barrier semaphores. Data moves between devices by JAX's collectives and lax.ppermute only.
A program may use at most 128 MiB of HBM per device.

```python
import jax
import jax.numpy as jnp
from jax import lax

D = 3584
HEADS = 28
KV_HEADS = 4
HD = 128
TOK_DEV = 128
TOKENS = 1024
CACHE = 2048
KEPT = 512


def draw_keep(key, part):
    ranks = TOKENS // TOK_DEV
    first_key, second_key, third_key = jax.random.split(jax.random.fold_in(key, 11), 3)
    weight = jax.random.randint(first_key, (ranks,), 1, 17)
    base = jax.random.randint(second_key, (TOKENS,), 0, 1024)
    owner = jnp.arange(TOKENS) // TOK_DEV
    full = jax.random.randint(third_key, (), 0, ranks)
    score = base * weight[owner] * TOKENS + jnp.arange(TOKENS)
    score = score + jnp.where(owner == full, 2 ** 30, 0)
    picked = lax.top_k(score.astype(jnp.int32), TOKENS // 2)[1]
    return jnp.zeros((TOKENS,), jnp.int32).at[picked].set(1)


def draw_cache_key(key, part):
    first_key = jax.random.fold_in(jax.random.fold_in(key, 23), 0)
    shape = (CACHE, KV_HEADS * HD)
    values = jnp.clip(jax.random.normal(first_key, shape, jnp.float32), -6.0, 6.0)
    return values.astype(jnp.bfloat16)


def place_ends(values, stream_key, smallest, largest):
    spot = [jax.random.randint(jax.random.fold_in(stream_key, axis), (), 0, length) for axis, length in enumerate(values.shape)]
    longest = values.shape.index(max(values.shape))
    next_to = spot[:longest] + [(spot[longest] + 1) % values.shape[longest]] + spot[longest + 1:]
    return values.at[tuple(spot)].set(smallest).at[tuple(next_to)].set(largest)


def block_levels(own_key, dims, cuts, least, high):
    level = 1.0
    for dim, blocks in cuts:
        steps = jax.random.uniform(jax.random.fold_in(jax.random.fold_in(own_key, 6), dim), (blocks,), jnp.float32, least / len(cuts), high / len(cuts))
        level = level * jnp.repeat(jnp.exp(steps), dims[dim] // blocks).reshape((-1,) + (1,) * (len(dims) - 1 - dim))
    return level


def centred(rng, extent, spread, limit, pieces=(), kind=jnp.bfloat16):
    drawn = jax.random.normal(rng, extent, jnp.float32) * spread
    if len(pieces) > 0:
        drawn = block_levels(rng, extent, pieces, -0.22, 0.18) * drawn
    return jnp.clip(drawn, min=-limit, max=limit).astype(kind)


def setup_inputs(seed: int = 0) -> dict:
    seeds = jax.random.split(jax.random.key(seed), 13)
    return {
        "hidden": centred(seeds[0], (TOKENS, D), 1.0, 6.0, ((0, 8), (1, 4))),
        "norm_gain": jnp.clip(1.0 + 0.18 * jax.random.normal(seeds[1], (D,), jnp.float32), 0.1, 1.9),
        "w_query": centred(seeds[2], (D, HEADS * HD), D ** -0.5, 0.09375, ((1, 4),)),
        "bias_query": centred(seeds[3], (HEADS * HD,), 0.5, 3.0, ((0, 4),), jnp.float32),
        "w_key": centred(seeds[4], (D, KV_HEADS * HD), D ** -0.5, 0.09375, ((1, 4),)),
        "bias_key": centred(seeds[5], (KV_HEADS * HD,), 0.5, 3.0, ((0, 4),), jnp.float32),
        "w_value": centred(seeds[6], (D, KV_HEADS * HD), D ** -0.5, 0.09375, ((1, 4),)),
        "bias_value": centred(seeds[7], (KV_HEADS * HD,), 0.5, 3.0, ((0, 4),), jnp.float32),
        "cache_key": draw_cache_key(jax.random.fold_in(seeds[12], 71), 0),
        "cache_value": centred(seeds[9], (CACHE, KV_HEADS * HD), 1.0, 6.0, ((0, 8), (1, 4))),
        "keep": draw_keep(jax.random.fold_in(seeds[12], 71), 0),
        "positions": place_ends(jax.random.randint(seeds[11], (3, TOKENS), 0, 2048), jax.random.fold_in(seeds[11], 1), 0, 2047).astype(jnp.int32),
    }


def rotate(flat, where):
    count = flat.shape[0]
    heads = flat.shape[1] // HD
    x = flat.reshape(count, heads, HD)
    half = HD // 2
    freq = jnp.arange(half)
    inv = jnp.exp(-(2.0 * freq.astype(jnp.float32) / HD) * jnp.log(jnp.float32(1000000.0)))
    section = jnp.where(freq < HD // 8, 0, jnp.where(freq < HD // 8 + 3 * HD // 16, 1, 2))
    picked = where[section, :].astype(jnp.float32).T
    angle = picked * inv[None, :]
    cosine = jnp.concatenate([jnp.cos(angle), jnp.cos(angle)], axis=1)[:, None, :]
    sine = jnp.concatenate([jnp.sin(angle), jnp.sin(angle)], axis=1)[:, None, :]
    turned = jnp.concatenate([-x[:, :, half:], x[:, :, :half]], axis=2)
    return x * cosine + turned * sine

def reference(hidden, norm_gain, w_query, bias_query, w_key, bias_key, w_value, bias_value, cache_key, cache_value, keep, positions):
    kept_index = jnp.nonzero(keep, size=KEPT)[0].astype(jnp.int32)
    rows = hidden[kept_index].astype(jnp.float32)
    scale_row = lax.rsqrt(lax.optimization_barrier(jnp.mean(rows * rows, axis=1, keepdims=True)) + 1e-06)
    normed = (rows * scale_row * norm_gain[None, :]).astype(jnp.bfloat16)
    where = positions[:, kept_index]
    query = rotate(jnp.dot(normed, w_query, preferred_element_type=jnp.float32) + bias_query, where).astype(jnp.bfloat16)
    fresh_key = rotate(jnp.dot(normed, w_key, preferred_element_type=jnp.float32) + bias_key, where).astype(jnp.bfloat16)
    fresh_value = (jnp.dot(normed, w_value, preferred_element_type=jnp.float32) + bias_value).astype(jnp.bfloat16)
    groups = HEADS // KV_HEADS
    keys = jnp.concatenate([cache_key.reshape(CACHE, KV_HEADS, HD), fresh_key], axis=0).astype(jnp.float32)
    values = jnp.concatenate([cache_value.reshape(CACHE, KV_HEADS, HD), fresh_value.reshape(KEPT, KV_HEADS, HD)], axis=0).astype(jnp.float32)
    key_place = jnp.concatenate([jnp.full((CACHE,), -1, jnp.int32), jnp.arange(KEPT, dtype=jnp.int32)])
    block = 256
    query_blocks = query.reshape(KEPT // block, block, KV_HEADS, groups, HD)
    query_order = jnp.arange(KEPT, dtype=jnp.int32).reshape(KEPT // block, block)
    factor = 1.0 / jnp.sqrt(jnp.float32(HD))

    def one_block(item):
        part_query, order = item
        score = jnp.einsum('qhgd,khd->hgqk', part_query.astype(jnp.float32), keys) * factor
        seen = key_place[None, :] <= order[:, None]
        score = jnp.where(seen[None, None], score, -jnp.inf)
        peak = lax.optimization_barrier(jnp.max(score, axis=-1, keepdims=True))
        weights = jnp.exp(score - peak)
        total = lax.optimization_barrier(jnp.sum(weights, axis=-1))
        rounded = weights.astype(jnp.bfloat16).astype(jnp.float32)
        summed = jnp.einsum('hgqk,khd->qhgd', rounded, values)
        return summed / jnp.transpose(total, (2, 0, 1))[..., None]
    result = lax.map(one_block, (query_blocks, query_order))
    result = result.reshape(KEPT, HEADS * HD).astype(jnp.bfloat16)
    return jnp.zeros((TOKENS, HEADS * HD), jnp.bfloat16).at[kept_index].set(result)
```

```python
import functools

import jax
import jax.numpy as jnp
from jax import lax
from jax.experimental import pallas as pl
from jax.experimental.pallas import tpu as pltpu
from jax.sharding import PartitionSpec as P

HD = 128
LOG2E = 1.4426950408889634


def swap(x, axis, n, k):
    return lax.ppermute(x, axis, [(i, i ^ k) for i in range(n)])


def flip(row):
    n = row.shape[1]
    eye = lax.broadcasted_iota(jnp.int32, (n, n), 0) == lax.broadcasted_iota(jnp.int32, (n, n), 1)
    return jnp.sum(jnp.where(eye, row, jnp.zeros_like(row)), axis=1, keepdims=True)


def start_copies(pairs, sems):
    copies = [pltpu.make_async_copy(a, b, sems.at[i]) for i, (a, b) in enumerate(pairs)]
    for copy in copies:
        copy.start()
    return copies


def setup_kernel(moved, rank_ref, keep_in, spots_in, key_in, value_in, *refs):
    sources, targets = refs[:moved], refs[moved : 2 * moved]
    stacked, cosine, sine, tags, order, live, keep, spots, sems = refs[2 * moved :]
    rank = rank_ref[0]
    copies = start_copies(
        [(keep_in, keep), (spots_in, spots), (key_in, stacked.at[0]), (value_in, stacked.at[1])]
        + list(zip(sources, targets)),
        sems,
    )
    copies[0].wait()
    copies[1].wait()
    blocks, rows = keep.shape
    kept = keep[...].astype(jnp.float32)
    upper = lax.broadcasted_iota(jnp.int32, (rows, rows), 0) < lax.broadcasted_iota(jnp.int32, (rows, rows), 1)
    inner = jnp.dot(kept.astype(jnp.bfloat16), upper.astype(jnp.bfloat16), preferred_element_type=jnp.float32)
    counts = jnp.broadcast_to(jnp.sum(kept, axis=1, keepdims=True), (blocks, rows))
    lower = lax.broadcasted_iota(jnp.int32, (blocks, blocks), 1) < lax.broadcasted_iota(jnp.int32, (blocks, blocks), 0)
    before = jnp.dot(lower.astype(jnp.bfloat16), counts.astype(jnp.bfloat16), preferred_element_type=jnp.float32)
    ordinals = inner + before
    tags[...] = jnp.where(kept > 0, ordinals, jnp.float32(2**30))
    mine = lax.broadcasted_iota(jnp.int32, (blocks, rows), 0) == rank
    order[...] = flip(jnp.sum(jnp.where(mine, ordinals, 0.0), axis=0, keepdims=True))
    live[...] = flip(jnp.sum(jnp.where(mine, kept, 0.0), axis=0, keepdims=True))

    where = spots[:, pl.ds(pl.multiple_of(rank * rows, rows), rows)].astype(jnp.float32)
    half = HD // 2
    freq = lax.rem(lax.broadcasted_iota(jnp.int32, (1, HD), 1), half)
    inv = jnp.exp(-(2.0 * freq.astype(jnp.float32) / HD) * jnp.log(jnp.full((1, 1), 1000000.0, jnp.float32)))
    picked = jnp.where(
        freq < HD // 8,
        flip(where[0:1]),
        jnp.where(freq < HD // 8 + 3 * HD // 16, flip(where[1:2]), flip(where[2:3])),
    )
    angle = picked * inv
    cosine[...] = jnp.cos(angle)
    low = lax.broadcasted_iota(jnp.int32, (1, HD), 1) < half
    sine[...] = jnp.where(low, -1.0, 1.0) * jnp.sin(angle)
    for copy in copies[2:]:
        copy.wait()


def turn(x, cosine, sine):
    return x * cosine + pltpu.roll(x, HD // 2, 1) * sine


def wide(ref, start, count):
    block = ref[pl.ds(start, count), :]
    return jnp.concatenate([block[i : i + 1] for i in range(count)], axis=1)


def key_value_kernel(parts, *refs):
    me_ref = refs[0]
    hidden_refs = refs[1 : 1 + parts]
    gain, w_key, bias_key, w_value, bias_value, cosine, sine, normed, fresh = refs[1 + parts :]
    width = hidden_refs[0].shape[1]
    me = me_ref[0]
    square = None
    for ref in hidden_refs:
        x = ref[...].astype(jnp.float32)
        part = jnp.sum(x * x, axis=1, keepdims=True)
        square = part if square is None else square + part
    scale = lax.rsqrt(square * (1.0 / (width * parts)) + 1e-06)
    key_sum = value_sum = None
    for j, ref in enumerate(hidden_refs):
        spot = pl.multiple_of((me ^ j) * width, width)
        x = ref[...].astype(jnp.float32)
        piece = (x * scale * wide(gain, (me ^ j) * (width // HD), width // HD)).astype(jnp.bfloat16)
        normed[:, j * width : (j + 1) * width] = piece
        k = jnp.dot(piece, w_key[pl.ds(spot, width), :], preferred_element_type=jnp.float32)
        v = jnp.dot(piece, w_value[pl.ds(spot, width), :], preferred_element_type=jnp.float32)
        key_sum = k if key_sum is None else key_sum + k
        value_sum = v if value_sum is None else value_sum + v
    for h in range(key_sum.shape[1] // HD):
        cut = slice(h * HD, (h + 1) * HD)
        fresh[0, :, cut] = turn(key_sum[:, cut] + bias_key[h : h + 1, :], cosine[...], sine[...]).astype(jnp.bfloat16)
        fresh[1, :, cut] = (value_sum[:, cut] + bias_value[h : h + 1, :]).astype(jnp.bfloat16)


def query_kernel(parts, me_ref, normed, weight, bias_query, cosine, sine, query, w_query, sems):
    width = normed.shape[1] // parts
    me = me_ref[0]
    spots = [pl.ds(pl.multiple_of((me ^ j) * width, width), width) for j in range(parts)]
    copies = start_copies([(weight.at[spot, :], w_query.at[j]) for j, spot in enumerate(spots)], sems)
    total = None
    for j in range(parts):
        copies[j].wait()
        q = jnp.dot(normed[:, j * width : (j + 1) * width], w_query[j], preferred_element_type=jnp.float32)
        total = q if total is None else total + q
    rows = normed.shape[0]
    for h in range(total.shape[1] // HD):
        cut = slice(h * HD, (h + 1) * HD)
        query[h * rows : (h + 1) * rows, :] = turn(
            total[:, cut] + bias_query[h : h + 1, :], cosine[...], sine[...]
        ).astype(jnp.bfloat16)


SCALE = LOG2E / (HD**0.5)


def absorb(state, query, key, value, seen):
    score = lax.dot_general(query, key, (((1,), (1,)), ((), ())), preferred_element_type=jnp.float32)
    if seen is not None:
        score = jnp.where(seen, score, -jnp.inf)
    higher = jnp.max(score, axis=1, keepdims=True)
    if state is not None:
        peak, total, summed = state
        higher = jnp.maximum(peak, higher)
    weights = jnp.exp2((score - higher) * SCALE)
    sums = jnp.sum(weights, axis=1, keepdims=True)
    added = jnp.dot(weights.astype(jnp.bfloat16), value, preferred_element_type=jnp.float32)
    if state is None:
        return higher, sums, added
    shrink = jnp.exp2((peak - higher) * SCALE)
    return higher, total * shrink + sums, summed * shrink + added


def chunks(refs, most):
    group = []
    for j, ref in enumerate(refs):
        group.append((j, ref))
        if len(group) * ref.shape[2] >= most or j == len(refs) - 1:
            yield group
            group = []


def attend_kernel(spans, given, last, *refs):
    refs = list(refs)
    rank_ref, query = refs.pop(0), refs.pop(0)
    masked = any(sources is not None for unused, sources in spans)
    if masked:
        tags, order = refs.pop(0), refs.pop(0)
    if last:
        live = refs.pop(0)
    state = None
    if given:
        peak, total, summed = refs.pop(0), refs.pop(0), refs.pop(0)
        state = (peak[...], total[...], summed[...])
    q = query[...]
    rank = rank_ref[0]
    for number, sources in spans:
        blocks, refs = refs[:number], refs[number:]
        rows = query.shape[0]
        if blocks[0].shape[0] > 1:
            ref = blocks[0]
            if state is None:
                state = (
                    jnp.full((rows, 1), -1e30, jnp.float32),
                    jnp.zeros((rows, 1), jnp.float32),
                    jnp.zeros((rows, HD), jnp.float32),
                )

            def step(i, carry):
                seen = None
                if sources is not None:
                    seen = jnp.concatenate([tags[pl.ds(i, 1), :] <= order[...]] * (rows // order.shape[0]), axis=0)
                return absorb(carry, q, ref[i, 0], ref[i, 1], seen)

            state = lax.fori_loop(0, ref.shape[0], step, state)
            continue
        for group in chunks(blocks, 1024):
            key = jnp.concatenate([ref[0, 0] for j, ref in group], axis=0)
            value = jnp.concatenate([ref[0, 1] for j, ref in group], axis=0)
            seen = None
            if sources is not None:
                tag = jnp.concatenate([tags[pl.ds(rank ^ sources[j], 1), :] for j, ref in group], axis=1)
                seen = jnp.concatenate([tag <= order[...]] * (rows // order.shape[0]), axis=0)
            state = absorb(state, q, key, value, seen)
    if not last:
        for ref, part in zip(refs, state):
            ref[...] = part
        return
    out = refs[0]
    count = out.shape[0]
    result = state[2] / state[1]
    for h in range(result.shape[0] // count):
        out[:, h * HD : (h + 1) * HD] = (result[h * count : (h + 1) * count] * live[...]).astype(jnp.bfloat16)


def call(kernel, outs, args, scalars=0, far=(), scratch=(), flops=0, moved=0):
    many = isinstance(outs, (list, tuple))
    specs = [pl.BlockSpec(memory_space=pltpu.SMEM)] * scalars
    specs += [
        pl.BlockSpec(memory_space=pltpu.HBM if i in far else pltpu.VMEM) for i in range(scalars, len(args))
    ]
    out_specs = jax.tree.map(lambda _: pl.BlockSpec(memory_space=pltpu.VMEM), list(outs) if many else outs)
    return pl.pallas_call(
        kernel,
        out_shape=list(outs) if many else outs,
        in_specs=specs,
        out_specs=out_specs,
        scratch_shapes=list(scratch),
        compiler_params=pltpu.CompilerParams(vmem_limit_bytes=40 * 1024 * 1024),
        cost_estimate=pl.CostEstimate(flops=flops, bytes_accessed=moved, transcendentals=0),
    )(*args)


def spread(x, n, near=True):
    return [x] + [swap(x, "ctx", n, k) for k in range(2, n, 2)]


def local(
    hidden,
    norm_gain,
    w_query,
    bias_query,
    w_key,
    bias_key,
    w_value,
    bias_value,
    cache_key,
    cache_value,
    keep,
    positions,
):
    n_ctx, n_tp = lax.axis_size("ctx"), lax.axis_size("tp")
    rank = lax.axis_index("ctx")[None].astype(jnp.int32)
    me = lax.axis_index("tp")[None].astype(jnp.int32)
    rows, width = hidden.shape
    kv_width = w_key.shape[1]
    heads = w_query.shape[1] // HD
    sds = jax.ShapeDtypeStruct
    f32, bf16 = jnp.float32, jnp.bfloat16
    small = n_ctx == 8

    pieces, order = [hidden], [0]
    step = n_tp // 2
    while step:
        pieces += [swap(p, "tp", n_tp, step) for p in pieces]
        order += [o ^ step for o in order]
        step //= 2
    pieces = [pieces[order.index(j)] for j in range(n_tp)]

    carried = (
        hidden,
        norm_gain.reshape(-1, HD),
        w_key,
        bias_key.reshape(-1, HD),
        w_value,
        bias_value.reshape(-1, HD),
        bias_query.reshape(-1, HD),
    )
    setup = call(
        functools.partial(setup_kernel, len(carried)),
        [sds(a.shape, a.dtype) for a in carried]
        + [
            sds((2, *cache_key.shape), bf16),
            sds((rows, HD), f32),
            sds((rows, HD), f32),
            sds((n_ctx, rows), f32),
            sds((rows, 1), f32),
            sds((rows, 1), f32),
        ],
        (rank, keep.reshape(n_ctx, rows), positions, cache_key, cache_value, *carried),
        1,
        range(1, 5 + len(carried)),
        [
            pltpu.VMEM((n_ctx, rows), jnp.int32),
            pltpu.VMEM(positions.shape, jnp.int32),
            pltpu.SemaphoreType.DMA((4 + len(carried),)),
        ],
        0,
        4000000,
    )
    pieces[0], gain, key_weight, key_bias, value_weight, value_bias, query_bias = setup[:7]
    cache, cosine, sine, tags, own_order, live = setup[7:]

    def pairs(x):
        return [swap(p, "ctx", n_ctx, 1) for p in x]

    if small:
        cache_near = spread(cache, n_ctx)
        cache_far = pairs(cache_near)

    normed, fresh = call(
        functools.partial(key_value_kernel, n_tp),
        (sds((rows, width * n_tp), bf16), sds((2, rows, kv_width), bf16)),
        (me, *pieces, gain, key_weight, key_bias, value_weight, value_bias, cosine, sine),
        1,
        flops=2 * rows * width * n_tp * 2 * kv_width,
        moved=3000000,
    )
    if small:
        fresh_near = spread(fresh, n_ctx)
        fresh_far = pairs(fresh_near)
    query = call(
        functools.partial(query_kernel, n_tp),
        sds((rows * heads, HD), bf16),
        (me, normed, w_query, query_bias, cosine, sine),
        1,
        (2,),
        [pltpu.VMEM((n_tp, width, heads * HD), bf16), pltpu.SemaphoreType.DMA((n_tp,))],
        2 * rows * width * n_tp * heads * HD,
        7000000,
    )
    shape = [sds((rows * heads, 1), f32), sds((rows * heads, 1), f32), sds((rows * heads, HD), f32)]
    final = sds((rows, heads * HD), bf16)

    def attend(spans, blocks, state=None, last=False):
        masked = any(s is not None for unused, s in spans)
        args = (rank, query)
        args += (tags, own_order) if masked else ()
        args += (live,) if last else ()
        args += tuple(state) if state is not None else ()
        keys = sum(b.shape[0] * b.shape[2] for b in blocks)
        return call(
            functools.partial(attend_kernel, spans, state is not None, last),
            final if last else shape,
            args + tuple(blocks),
            1,
            flops=4 * rows * heads * HD * keys,
            moved=16 * rows * heads * keys,
        )

    if not small:
        cached = lax.all_gather(cache, "ctx", axis=0)
        news = lax.all_gather(fresh, "ctx", axis=0)
        state = attend([(1, None)], [cached])
        return attend([(1, (0,))], [news], state, True)
    near, far = tuple(range(0, n_ctx, 2)), tuple(range(1, n_ctx, 2))
    count = n_ctx // 2
    block = lambda x: [p[None] for p in x]
    state = attend([(count, None)], block(cache_near))
    state = attend([(count, None), (count, near)], block(cache_far) + block(fresh_near), state)
    return attend([(count, far)], block(fresh_far), state, True)


def solution(mesh):
    in_specs = (
        P("ctx", "tp"),
        P(),
        P(None, "tp"),
        P("tp"),
        P(None, "tp"),
        P("tp"),
        P(None, "tp"),
        P("tp"),
        P("ctx", "tp"),
        P("ctx", "tp"),
        P(),
        P(),
    )
    return jax.shard_map(local, mesh=mesh, in_specs=in_specs, out_specs=P("ctx", "tp"), check_vma=False)
```

```python
import functools

import jax
import jax.numpy as jnp
from jax import lax
from jax.experimental import pallas as pl
from jax.experimental.pallas import tpu as pltpu
from jax.sharding import PartitionSpec as P


HD = 128
LOG2E = 1.4426950408889634

EARLY = 4


def swap(x, axis, n, k):
    return lax.ppermute(x, axis, [(i, i ^ k) for i in range(n)])


def flip(row):
    n = row.shape[1]
    eye = lax.broadcasted_iota(jnp.int32, (n, n), 0) == lax.broadcasted_iota(jnp.int32, (n, n), 1)
    return jnp.sum(jnp.where(eye, row, jnp.zeros_like(row)), axis=1, keepdims=True)


def start_copies(pairs, sems):
    copies = [pltpu.make_async_copy(a, b, sems.at[i]) for i, (a, b) in enumerate(pairs)]
    for copy in copies:
        copy.start()
    return copies


def stack_kernel(key_in, value_in, stacked, sems):
    for copy in start_copies([(key_in, stacked.at[0]), (value_in, stacked.at[1])], sems):
        copy.wait()


def part_of(weight, me, j, parts):
    depth = weight.shape[0] // parts
    return weight.at[pl.ds(pl.multiple_of((me ^ j) * depth, depth), depth), :]


def setup_kernel(moved, parts, rank_ref, me_ref, keep_in, spots_in, w_query, *refs):
    sources, targets = refs[:moved], refs[moved : 2 * moved]
    weights, refs = refs[2 * moved : 2 * moved + EARLY], refs[2 * moved + EARLY :]
    cosine, sine, tags, order, live, keep, spots, sems = refs
    rank = rank_ref[0]
    copies = start_copies(
        [(keep_in, keep), (spots_in, spots)]
        + list(zip(sources, targets))
        + [(part_of(w_query, me_ref[0], j, parts), weight) for j, weight in enumerate(weights)],
        sems,
    )
    copies[0].wait()
    copies[1].wait()
    blocks, rows = keep.shape
    kept = keep[...].astype(jnp.float32)
    upper = lax.broadcasted_iota(jnp.int32, (rows, rows), 0) < lax.broadcasted_iota(jnp.int32, (rows, rows), 1)
    inner = jnp.dot(kept.astype(jnp.bfloat16), upper.astype(jnp.bfloat16), preferred_element_type=jnp.float32)
    counts = jnp.broadcast_to(jnp.sum(kept, axis=1, keepdims=True), (blocks, rows))
    lower = lax.broadcasted_iota(jnp.int32, (blocks, blocks), 1) < lax.broadcasted_iota(jnp.int32, (blocks, blocks), 0)
    before = jnp.dot(lower.astype(jnp.bfloat16), counts.astype(jnp.bfloat16), preferred_element_type=jnp.float32)
    ordinals = inner + before
    tags[...] = jnp.where(kept > 0, ordinals, jnp.float32(2**30))
    mine = lax.broadcasted_iota(jnp.int32, (blocks, rows), 0) == rank
    order[...] = flip(jnp.sum(jnp.where(mine, ordinals, 0.0), axis=0, keepdims=True))
    live[...] = flip(jnp.sum(jnp.where(mine, kept, 0.0), axis=0, keepdims=True))

    where = spots[:, pl.ds(pl.multiple_of(rank * rows, rows), rows)].astype(jnp.float32)
    half = HD // 2
    freq = lax.rem(lax.broadcasted_iota(jnp.int32, (1, HD), 1), half)
    inv = jnp.exp(-(2.0 * freq.astype(jnp.float32) / HD) * jnp.log(jnp.full((1, 1), 1000000.0, jnp.float32)))
    picked = jnp.where(
        freq < HD // 8,
        flip(where[0:1]),
        jnp.where(freq < HD // 8 + 3 * HD // 16, flip(where[1:2]), flip(where[2:3])),
    )
    angle = picked * inv
    cosine[...] = jnp.cos(angle)
    low = lax.broadcasted_iota(jnp.int32, (1, HD), 1) < half
    sine[...] = jnp.where(low, -1.0, 1.0) * jnp.sin(angle)
    for copy in copies[2:]:
        copy.wait()


def turn(x, cosine, sine):
    return x * cosine + pltpu.roll(x, HD // 2, 1) * sine


def wide(ref, start, count):
    block = ref[pl.ds(start, count), :]
    return jnp.concatenate([block[i : i + 1] for i in range(count)], axis=1)


def key_value_kernel(parts, *refs):
    me_ref = refs[0]
    hidden_refs = refs[1 : 1 + parts]
    gain, w_key, bias_key, w_value, bias_value, cosine, sine, normed, fresh = refs[1 + parts :]
    width = hidden_refs[0].shape[1]
    me = me_ref[0]
    square = None
    for ref in hidden_refs:
        x = ref[...].astype(jnp.float32)
        part = jnp.sum(x * x, axis=1, keepdims=True)
        square = part if square is None else square + part
    scale = lax.rsqrt(square * (1.0 / (width * parts)) + 1e-06)
    key_sum = value_sum = None
    for j, ref in enumerate(hidden_refs):
        spot = pl.multiple_of((me ^ j) * width, width)
        x = ref[...].astype(jnp.float32)
        piece = (x * scale * wide(gain, (me ^ j) * (width // HD), width // HD)).astype(jnp.bfloat16)
        normed[:, j * width : (j + 1) * width] = piece
        k = jnp.dot(piece, w_key[pl.ds(spot, width), :], preferred_element_type=jnp.float32)
        v = jnp.dot(piece, w_value[pl.ds(spot, width), :], preferred_element_type=jnp.float32)
        key_sum = k if key_sum is None else key_sum + k
        value_sum = v if value_sum is None else value_sum + v
    for h in range(key_sum.shape[1] // HD):
        cut = slice(h * HD, (h + 1) * HD)
        fresh[0, :, cut] = turn(key_sum[:, cut] + bias_key[h : h + 1, :], cosine[...], sine[...]).astype(jnp.bfloat16)
        fresh[1, :, cut] = (value_sum[:, cut] + bias_value[h : h + 1, :]).astype(jnp.bfloat16)


def query_kernel(parts, me_ref, normed, bias_query, cosine, sine, w_query, *refs):
    early, query = refs[:EARLY], refs[EARLY]
    width = normed.shape[1] // parts
    late = range(EARLY, parts)
    if late:
        weights, sems = refs[EARLY + 1 :]
        copies = start_copies([(part_of(w_query, me_ref[0], j, parts), weights.at[j - EARLY]) for j in late], sems)
    total = None
    for j in range(parts):
        if j >= EARLY:
            copies[j - EARLY].wait()
        weight = early[j][...] if j < EARLY else weights[j - EARLY]
        q = jnp.dot(normed[:, j * width : (j + 1) * width], weight, preferred_element_type=jnp.float32)
        total = q if total is None else total + q
    rows = normed.shape[0]
    for h in range(total.shape[1] // HD):
        cut = slice(h * HD, (h + 1) * HD)
        query[h * rows : (h + 1) * rows, :] = turn(
            total[:, cut] + bias_query[h : h + 1, :], cosine[...], sine[...]
        ).astype(jnp.bfloat16)


SCALE = LOG2E / (HD**0.5)


def fold(x):
    out = x[:, :HD]
    for spot in range(HD, x.shape[1], HD):
        out = out + x[:, spot : spot + HD]
    return out


def absorb(state, query, key, value, bias):
    rows, count = query.shape[0], key.shape[0]
    score = lax.dot_general(query, key, (((1,), (1,)), ((), ())), preferred_element_type=jnp.float32)
    if bias is not None:
        own = bias.shape[0]
        score = jnp.concatenate([score[r : r + own] + bias for r in range(0, rows, own)], axis=0)
    higher = jnp.broadcast_to(jnp.max(score, axis=1, keepdims=True), (rows, HD))
    if state is not None:
        peak, total, summed = state
        higher = jnp.maximum(peak, higher)
    weights = jnp.exp2((score - jnp.concatenate([higher] * (count // HD), axis=1)) * SCALE)
    sums = fold(weights)
    added = jnp.dot(weights.astype(jnp.bfloat16), value, preferred_element_type=jnp.float32)
    if state is None:
        return higher, sums, added
    shrink = jnp.exp2((peak - higher) * SCALE)
    return higher, total * shrink + sums, summed * shrink + added


def groups(segments):
    group, count = [], 0
    for segment in segments:
        group.append(segment)
        count += segment[2]
        if count >= CHUNK or segment is segments[-1]:
            yield group
            group, count = [], 0


def attend_kernel(segments, given, last, *refs):
    refs = list(refs)
    rank, query, tags, order, live = refs[0][0], *refs[1:5]
    del refs[:5]
    state = None
    if given:
        state = tuple(ref[...] for ref in refs[:3])
        del refs[:3]
    q = query[...]
    for fresh in (False, True):
        for group in groups([s for s in segments if (s[3] is not None) == fresh]):
            key, value = [
                jnp.concatenate([refs[i][kind, start : start + count] for i, start, count, unused in group], axis=0)
                for kind in range(2)
            ]
            bias = None
            if fresh:
                tag = jnp.concatenate([tags[pl.ds(rank ^ s[3], 1), :] for s in group], axis=1)
                bias = jnp.where(tag <= order[...], 0.0, -jnp.inf)
            state = absorb(state, q, key, value, bias)
    finish(refs[len({s[0] for s in segments}) :], state, live, last)


def join_kernel(cuts, *refs):
    spot = 0
    for ref, (start, count) in zip(refs, cuts):
        refs[-1][:, spot : spot + count] = ref[:, start : start + count]
        spot += count


def finish(refs, state, live, last):
    if not last:
        for ref, part in zip(refs, state):
            ref[...] = part
        return
    out = refs[0]
    count = out.shape[0]
    result = state[2] * (1.0 / jnp.sum(state[1], axis=1, keepdims=True))
    for h in range(result.shape[0] // count):
        out[:, h * HD : (h + 1) * HD] = (result[h * count : (h + 1) * count] * live[...]).astype(jnp.bfloat16)


def stacked_kernel(query, tags, order, live, cached, news, out):
    rows = query.shape[0]
    q = query[...]

    def plain(i, state):
        return absorb(state, q, cached[i, 0], cached[i, 1], None)

    def masked(i, state):
        bias = jnp.where(tags[pl.ds(i, 1), :] <= order[...], 0.0, -jnp.inf)
        return absorb(state, q, news[i, 0], news[i, 1], bias)

    state = (
        jnp.full((rows, HD), -1e30, jnp.float32),
        jnp.zeros((rows, HD), jnp.float32),
        jnp.zeros((rows, HD), jnp.float32),
    )
    state = lax.fori_loop(0, cached.shape[0], plain, state)
    state = lax.fori_loop(0, news.shape[0], masked, state)
    finish([out], state, live, True)


CHUNK = 512


def call(kernel, outs, args, scalars=0, far=(), scratch=(), flops=0, moved=0):
    many = isinstance(outs, (list, tuple))
    specs = [pl.BlockSpec(memory_space=pltpu.SMEM)] * scalars
    specs += [
        pl.BlockSpec(memory_space=pltpu.HBM if i in far else pltpu.VMEM) for i in range(scalars, len(args))
    ]
    out_specs = jax.tree.map(lambda _: pl.BlockSpec(memory_space=pltpu.VMEM), list(outs) if many else outs)
    args = [pltpu.with_memory_space_constraint(a, pltpu.HBM) if i in far else a for i, a in enumerate(args)]
    return pl.pallas_call(
        kernel,
        out_shape=list(outs) if many else outs,
        in_specs=specs,
        out_specs=out_specs,
        scratch_shapes=list(scratch),
        compiler_params=pltpu.CompilerParams(vmem_limit_bytes=20 * 1024 * 1024),
        cost_estimate=pl.CostEstimate(flops=flops, bytes_accessed=moved, transcendentals=0),
    )(*args)


def local(
    hidden,
    norm_gain,
    w_query,
    bias_query,
    w_key,
    bias_key,
    w_value,
    bias_value,
    cache_key,
    cache_value,
    keep,
    positions,
):
    n_ctx, n_tp = lax.axis_size("ctx"), lax.axis_size("tp")
    rank = lax.axis_index("ctx")[None].astype(jnp.int32)
    me = lax.axis_index("tp")[None].astype(jnp.int32)
    rows, width = hidden.shape
    kv_width = w_key.shape[1]
    heads = w_query.shape[1] // HD
    sds = jax.ShapeDtypeStruct
    f32, bf16 = jnp.float32, jnp.bfloat16

    far_hidden = swap(hidden, "tp", n_tp, 2)
    pieces = [hidden, swap(hidden, "tp", n_tp, 1), far_hidden, swap(far_hidden, "tp", n_tp, 1)]

    carried = (
        hidden,
        norm_gain.reshape(-1, HD),
        w_key,
        bias_key.reshape(-1, HD),
        w_value,
        bias_value.reshape(-1, HD),
        bias_query.reshape(-1, HD),
    )
    cache = call(
        stack_kernel,
        sds((2, *cache_key.shape), bf16),
        (cache_key, cache_value),
        far=(0, 1),
        scratch=[pltpu.SemaphoreType.DMA((2,))],
        moved=1000000,
    )
    setup = call(
        functools.partial(setup_kernel, len(carried), n_tp),
        [sds(a.shape, a.dtype) for a in carried]
        + [sds((width, heads * HD), bf16)] * EARLY
        + [
            sds((rows, HD), f32),
            sds((rows, HD), f32),
            sds((n_ctx, rows), f32),
            sds((rows, 1), f32),
            sds((rows, 1), f32),
        ],
        (rank, me, keep.reshape(n_ctx, rows), positions, w_query, *carried),
        2,
        range(2, 5 + len(carried)),
        [
            pltpu.VMEM((n_ctx, rows), jnp.int32),
            pltpu.VMEM(positions.shape, jnp.int32),
            pltpu.SemaphoreType.DMA((2 + EARLY + len(carried),)),
        ],
        0,
        4000000,
    )
    pieces[0], gain, key_weight, key_bias, value_weight, value_bias, query_bias = setup[:7]
    early = setup[7 : 7 + EARLY]
    cosine, sine, tags, own_order, live = setup[7 + EARLY :]

    normed, fresh = call(
        functools.partial(key_value_kernel, n_tp),
        (sds((rows, width * n_tp), bf16), sds((2, rows, kv_width), bf16)),
        (me, *pieces, gain, key_weight, key_bias, value_weight, value_bias, cosine, sine),
        1,
        flops=2 * rows * width * n_tp * 2 * kv_width,
        moved=3000000,
    )
    late = ()
    if n_tp > EARLY:
        late = (pltpu.VMEM((n_tp - EARLY, width, heads * HD), bf16), pltpu.SemaphoreType.DMA((n_tp - EARLY,)))
    query = call(
        functools.partial(query_kernel, n_tp),
        sds((rows * heads, HD), bf16),
        (me, normed, query_bias, cosine, sine, w_query, *early),
        1,
        (5,),
        late,
        flops=2 * rows * width * n_tp * heads * HD,
        moved=7000000,
    )
    final = sds((rows, heads * HD), bf16)
    if not paired(n_ctx):
        cached = lax.all_gather(cache, "ctx", axis=0)
        news = lax.all_gather(fresh, "ctx", axis=0)
        return call(stacked_kernel, final, (query, tags, own_order, live, cached, news))

    def attend(segments, state=None, last=False):
        arrays = []
        for array, *unused in segments:
            if not any(array is a for a in arrays):
                arrays.append(array)
        place = lambda array: [array is a for a in arrays].index(True)
        cuts = tuple((place(a), start, count, source) for a, start, count, source in segments)
        keys = sum(s[2] for s in segments)
        return call(
            functools.partial(attend_kernel, cuts, state is not None, last),
            final if last else [sds((rows * heads, HD), f32)] * 3,
            (rank, query, tags, own_order, live, *(state or ()), *arrays),
            1,
            flops=4 * rows * heads * HD * keys,
            moved=8 * rows * heads * keys,
        )

    def join(*cuts):
        out = sds((2, sum(c[2] for c in cuts), HD), bf16)
        return call(functools.partial(join_kernel, [c[1:] for c in cuts]), out, [c[0] for c in cuts])

    ctx = lambda x, k: swap(x, "ctx", n_ctx, k)
    old, new = cache.shape[1], rows
    c4 = ctx(cache, 4)
    c2 = ctx(cache, 2)
    c1 = ctx(cache, 1)
    c3 = ctx(c2, 1)
    c6 = ctx(c4, 2)
    f4 = ctx(fresh, 4)
    f2 = ctx(fresh, 2)
    f6 = ctx(f4, 2)
    ux = ctx(join((fresh, 0, new), (c4, 0, old)), 1)
    xa = ctx(join((f2, 0, new), (c6, 0, old)), 1)
    xb = ctx(join((f4, 0, new), (f6, 0, new)), 1)
    state = attend([(c, 0, old, None) for c in (cache, c2, c4, c1)])
    state = attend(
        [(c3, 0, old, None), (ux, new, old, None), (c6, 0, old, None)]
        + [(fresh, 0, new, 0), (ux, 0, new, 1), (f2, 0, new, 2), (f4, 0, new, 4), (f6, 0, new, 6)],
        state,
    )
    return attend([(xa, new, old, None), (xa, 0, new, 3), (xb, 0, new, 5), (xb, new, new, 7)], state, True)


def paired(n_ctx):
    return n_ctx == 8


def solution(mesh):
    in_specs = (
        P("ctx", "tp"),
        P(),
        P(None, "tp"),
        P("tp"),
        P(None, "tp"),
        P("tp"),
        P(None, "tp"),
        P("tp"),
        P("ctx", "tp"),
        P("ctx", "tp"),
        P(),
        P(),
    )

    return jax.shard_map(local, mesh=mesh, in_specs=in_specs, out_specs=P("ctx", "tp"), check_vma=False)
```

```python
import functools

import jax
import jax.numpy as jnp
from jax import lax
from jax.experimental import pallas as pl
from jax.experimental.pallas import tpu as pltpu
from jax.sharding import PartitionSpec as P


HD = 128
LOG2E = 1.4426950408889634

EARLY = 4


def swap(x, axis, n, k):
    return lax.ppermute(x, axis, [(i, i ^ k) for i in range(n)])


def flip(row):
    n = row.shape[1]
    eye = lax.broadcasted_iota(jnp.int32, (n, n), 0) == lax.broadcasted_iota(jnp.int32, (n, n), 1)
    return jnp.sum(jnp.where(eye, row, jnp.zeros_like(row)), axis=1, keepdims=True)


def start_copies(pairs, sems):
    copies = [pltpu.make_async_copy(a, b, sems.at[i]) for i, (a, b) in enumerate(pairs)]
    for copy in copies:
        copy.start()
    return copies


def stack_kernel(key_in, value_in, stacked, sems):
    for copy in start_copies([(key_in, stacked.at[0]), (value_in, stacked.at[1])], sems):
        copy.wait()


def part_of(weight, me, j, parts):
    depth = weight.shape[0] // parts
    return weight.at[pl.ds(pl.multiple_of((me ^ j) * depth, depth), depth), :]


def setup_kernel(moved, parts, rank_ref, me_ref, keep_in, spots_in, w_query, *refs):
    sources, targets = refs[:moved], refs[moved : 2 * moved]
    weights, refs = refs[2 * moved : 2 * moved + EARLY], refs[2 * moved + EARLY :]
    cosine, sine, tags, order, live, keep, spots, sems = refs
    rank = rank_ref[0]
    copies = start_copies(
        [(keep_in, keep), (spots_in, spots)]
        + list(zip(sources, targets))
        + [(part_of(w_query, me_ref[0], j, parts), weight) for j, weight in enumerate(weights)],
        sems,
    )
    copies[0].wait()
    copies[1].wait()
    blocks, rows = keep.shape
    kept = keep[...].astype(jnp.float32)
    upper = lax.broadcasted_iota(jnp.int32, (rows, rows), 0) < lax.broadcasted_iota(jnp.int32, (rows, rows), 1)
    inner = jnp.dot(kept.astype(jnp.bfloat16), upper.astype(jnp.bfloat16), preferred_element_type=jnp.float32)
    counts = jnp.broadcast_to(jnp.sum(kept, axis=1, keepdims=True), (blocks, rows))
    lower = lax.broadcasted_iota(jnp.int32, (blocks, blocks), 1) < lax.broadcasted_iota(jnp.int32, (blocks, blocks), 0)
    before = jnp.dot(lower.astype(jnp.bfloat16), counts.astype(jnp.bfloat16), preferred_element_type=jnp.float32)
    ordinals = inner + before
    tags[...] = jnp.where(kept > 0, ordinals, jnp.float32(2**30))
    mine = lax.broadcasted_iota(jnp.int32, (blocks, rows), 0) == rank
    order[...] = flip(jnp.sum(jnp.where(mine, ordinals, 0.0), axis=0, keepdims=True))
    live[...] = flip(jnp.sum(jnp.where(mine, kept, 0.0), axis=0, keepdims=True))

    where = spots[:, pl.ds(pl.multiple_of(rank * rows, rows), rows)].astype(jnp.float32)
    half = HD // 2
    freq = lax.rem(lax.broadcasted_iota(jnp.int32, (1, HD), 1), half)
    inv = jnp.exp(-(2.0 * freq.astype(jnp.float32) / HD) * jnp.log(jnp.full((1, 1), 1000000.0, jnp.float32)))
    picked = jnp.where(
        freq < HD // 8,
        flip(where[0:1]),
        jnp.where(freq < HD // 8 + 3 * HD // 16, flip(where[1:2]), flip(where[2:3])),
    )
    angle = picked * inv
    cosine[...] = jnp.cos(angle)
    low = lax.broadcasted_iota(jnp.int32, (1, HD), 1) < half
    sine[...] = jnp.where(low, -1.0, 1.0) * jnp.sin(angle)
    for copy in copies[2:]:
        copy.wait()


def turn(x, cosine, sine):
    return x * cosine + pltpu.roll(x, HD // 2, 1) * sine


def wide(ref, start, count):
    block = ref[pl.ds(start, count), :]
    return jnp.concatenate([block[i : i + 1] for i in range(count)], axis=1)


def key_value_kernel(parts, *refs):
    me_ref = refs[0]
    hidden_refs = refs[1 : 1 + parts]
    gain, w_key, bias_key, w_value, bias_value, cosine, sine, normed, fresh = refs[1 + parts :]
    width = hidden_refs[0].shape[1]
    me = me_ref[0]
    square = None
    for ref in hidden_refs:
        x = ref[...].astype(jnp.float32)
        part = jnp.sum(x * x, axis=1, keepdims=True)
        square = part if square is None else square + part
    scale = lax.rsqrt(square * (1.0 / (width * parts)) + 1e-06)
    key_sum = value_sum = None
    for j, ref in enumerate(hidden_refs):
        spot = pl.multiple_of((me ^ j) * width, width)
        x = ref[...].astype(jnp.float32)
        piece = (x * scale * wide(gain, (me ^ j) * (width // HD), width // HD)).astype(jnp.bfloat16)
        normed[:, j * width : (j + 1) * width] = piece
        k = jnp.dot(piece, w_key[pl.ds(spot, width), :], preferred_element_type=jnp.float32)
        v = jnp.dot(piece, w_value[pl.ds(spot, width), :], preferred_element_type=jnp.float32)
        key_sum = k if key_sum is None else key_sum + k
        value_sum = v if value_sum is None else value_sum + v
    for h in range(key_sum.shape[1] // HD):
        cut = slice(h * HD, (h + 1) * HD)
        fresh[0, :, cut] = turn(key_sum[:, cut] + bias_key[h : h + 1, :], cosine[...], sine[...]).astype(jnp.bfloat16)
        fresh[1, :, cut] = (value_sum[:, cut] + bias_value[h : h + 1, :]).astype(jnp.bfloat16)


def query_kernel(parts, me_ref, normed, bias_query, cosine, sine, w_query, *refs):
    early, query = refs[:EARLY], refs[EARLY]
    width = normed.shape[1] // parts
    late = range(EARLY, parts)
    if late:
        weights, sems = refs[EARLY + 1 :]
        copies = start_copies([(part_of(w_query, me_ref[0], j, parts), weights.at[j - EARLY]) for j in late], sems)
    total = None
    for j in range(parts):
        if j >= EARLY:
            copies[j - EARLY].wait()
        weight = early[j][...] if j < EARLY else weights[j - EARLY]
        q = jnp.dot(normed[:, j * width : (j + 1) * width], weight, preferred_element_type=jnp.float32)
        total = q if total is None else total + q
    rows = normed.shape[0]
    for h in range(total.shape[1] // HD):
        cut = slice(h * HD, (h + 1) * HD)
        query[h * rows : (h + 1) * rows, :] = turn(
            total[:, cut] + bias_query[h : h + 1, :], cosine[...], sine[...]
        ).astype(jnp.bfloat16)


SCALE = LOG2E / (HD**0.5)


def fold(x):
    out = x[:, :HD]
    for spot in range(HD, x.shape[1], HD):
        out = out + x[:, spot : spot + HD]
    return out


def absorb(state, query, key, value, bias):
    rows, count = query.shape[0], key.shape[0]
    score = lax.dot_general(query, key, (((1,), (1,)), ((), ())), preferred_element_type=jnp.float32)
    if bias is not None:
        own = bias.shape[0]
        score = jnp.concatenate([score[r : r + own] + bias for r in range(0, rows, own)], axis=0)
    higher = jnp.broadcast_to(jnp.max(score, axis=1, keepdims=True), (rows, HD))
    if state is not None:
        peak, total, summed = state
        higher = jnp.maximum(peak, higher)
    weights = jnp.exp2((score - jnp.concatenate([higher] * (count // HD), axis=1)) * SCALE)
    sums = fold(weights)
    added = jnp.dot(weights.astype(jnp.bfloat16), value, preferred_element_type=jnp.float32)
    if state is None:
        return higher, sums, added
    shrink = jnp.exp2((peak - higher) * SCALE)
    return higher, total * shrink + sums, summed * shrink + added


def groups(segments):
    group, count = [], 0
    for segment in segments:
        group.append(segment)
        count += segment[2]
        if count >= CHUNK or segment is segments[-1]:
            yield group
            group, count = [], 0


def attend_kernel(segments, given, last, *refs):
    refs = list(refs)
    rank, query, tags, order, live = refs[0][0], *refs[1:5]
    del refs[:5]
    state = None
    if given:
        state = tuple(ref[...] for ref in refs[:3])
        del refs[:3]
    q = query[...]
    for fresh in (False, True):
        for group in groups([s for s in segments if (s[3] is not None) == fresh]):
            key, value = [
                jnp.concatenate([refs[i][kind, start : start + count] for i, start, count, unused in group], axis=0)
                for kind in range(2)
            ]
            bias = None
            if fresh:
                tag = jnp.concatenate([tags[pl.ds(rank ^ s[3], 1), :] for s in group], axis=1)
                bias = jnp.where(tag <= order[...], 0.0, -jnp.inf)
            state = absorb(state, q, key, value, bias)
    finish(refs[len({s[0] for s in segments}) :], state, live, last)


def join_kernel(cuts, *refs):
    spot = 0
    for ref, (start, count) in zip(refs, cuts):
        refs[-1][:, spot : spot + count] = ref[:, start : start + count]
        spot += count


def finish(refs, state, live, last):
    if not last:
        for ref, part in zip(refs, state):
            ref[...] = part
        return
    out = refs[0]
    count = out.shape[0]
    result = state[2] * (1.0 / jnp.sum(state[1], axis=1, keepdims=True))
    for h in range(result.shape[0] // count):
        out[:, h * HD : (h + 1) * HD] = (result[h * count : (h + 1) * count] * live[...]).astype(jnp.bfloat16)


def stacked_kernel(query, tags, order, live, cached, news, out):
    rows = query.shape[0]
    q = query[...]

    def plain(i, state):
        return absorb(state, q, cached[i, 0], cached[i, 1], None)

    def masked(i, state):
        bias = jnp.where(tags[pl.ds(i, 1), :] <= order[...], 0.0, -jnp.inf)
        return absorb(state, q, news[i, 0], news[i, 1], bias)

    state = (
        jnp.full((rows, HD), -1e30, jnp.float32),
        jnp.zeros((rows, HD), jnp.float32),
        jnp.zeros((rows, HD), jnp.float32),
    )
    state = lax.fori_loop(0, cached.shape[0], plain, state)
    state = lax.fori_loop(0, news.shape[0], masked, state)
    finish([out], state, live, True)


CHUNK = 512


def call(kernel, outs, args, scalars=0, far=(), scratch=(), flops=0, moved=0):
    many = isinstance(outs, (list, tuple))
    specs = [pl.BlockSpec(memory_space=pltpu.SMEM)] * scalars
    specs += [
        pl.BlockSpec(memory_space=pltpu.HBM if i in far else pltpu.VMEM) for i in range(scalars, len(args))
    ]
    out_specs = jax.tree.map(lambda _: pl.BlockSpec(memory_space=pltpu.VMEM), list(outs) if many else outs)
    args = [pltpu.with_memory_space_constraint(a, pltpu.HBM) if i in far else a for i, a in enumerate(args)]
    return pl.pallas_call(
        kernel,
        out_shape=list(outs) if many else outs,
        in_specs=specs,
        out_specs=out_specs,
        scratch_shapes=list(scratch),
        compiler_params=pltpu.CompilerParams(vmem_limit_bytes=20 * 1024 * 1024),
        cost_estimate=pl.CostEstimate(flops=flops, bytes_accessed=moved, transcendentals=0),
    )(*args)


def local(
    hidden,
    norm_gain,
    w_query,
    bias_query,
    w_key,
    bias_key,
    w_value,
    bias_value,
    cache_key,
    cache_value,
    keep,
    positions,
):
    n_ctx, n_tp = lax.axis_size("ctx"), lax.axis_size("tp")
    rank = lax.axis_index("ctx")[None].astype(jnp.int32)
    me = lax.axis_index("tp")[None].astype(jnp.int32)
    rows, width = hidden.shape
    kv_width = w_key.shape[1]
    heads = w_query.shape[1] // HD
    sds = jax.ShapeDtypeStruct
    f32, bf16 = jnp.float32, jnp.bfloat16

    far_hidden = swap(hidden, "tp", n_tp, 2)
    pieces = [hidden, swap(hidden, "tp", n_tp, 1), far_hidden, swap(far_hidden, "tp", n_tp, 1)]

    carried = (
        hidden,
        norm_gain.reshape(-1, HD),
        w_key,
        bias_key.reshape(-1, HD),
        w_value,
        bias_value.reshape(-1, HD),
        bias_query.reshape(-1, HD),
    )
    cache = call(
        stack_kernel,
        sds((2, *cache_key.shape), bf16),
        (cache_key, cache_value),
        far=(0, 1),
        scratch=[pltpu.SemaphoreType.DMA((2,))],
        moved=1000000,
    )
    setup = call(
        functools.partial(setup_kernel, len(carried), n_tp),
        [sds(a.shape, a.dtype) for a in carried]
        + [sds((width, heads * HD), bf16)] * EARLY
        + [
            sds((rows, HD), f32),
            sds((rows, HD), f32),
            sds((n_ctx, rows), f32),
            sds((rows, 1), f32),
            sds((rows, 1), f32),
        ],
        (rank, me, keep.reshape(n_ctx, rows), positions, w_query, *carried),
        2,
        range(2, 5 + len(carried)),
        [
            pltpu.VMEM((n_ctx, rows), jnp.int32),
            pltpu.VMEM(positions.shape, jnp.int32),
            pltpu.SemaphoreType.DMA((2 + EARLY + len(carried),)),
        ],
        0,
        4000000,
    )
    pieces[0], gain, key_weight, key_bias, value_weight, value_bias, query_bias = setup[:7]
    early = setup[7 : 7 + EARLY]
    cosine, sine, tags, own_order, live = setup[7 + EARLY :]

    normed, fresh = call(
        functools.partial(key_value_kernel, n_tp),
        (sds((rows, width * n_tp), bf16), sds((2, rows, kv_width), bf16)),
        (me, *pieces, gain, key_weight, key_bias, value_weight, value_bias, cosine, sine),
        1,
        flops=2 * rows * width * n_tp * 2 * kv_width,
        moved=3000000,
    )
    late = ()
    if n_tp > EARLY:
        late = (pltpu.VMEM((n_tp - EARLY, width, heads * HD), bf16), pltpu.SemaphoreType.DMA((n_tp - EARLY,)))
    query = call(
        functools.partial(query_kernel, n_tp),
        sds((rows * heads, HD), bf16),
        (me, normed, query_bias, cosine, sine, w_query, *early),
        1,
        (5,),
        late,
        flops=2 * rows * width * n_tp * heads * HD,
        moved=7000000,
    )
    final = sds((rows, heads * HD), bf16)
    if not paired(n_ctx):
        cached = lax.all_gather(cache, "ctx", axis=0)
        news = lax.all_gather(fresh, "ctx", axis=0)
        return call(stacked_kernel, final, (query, tags, own_order, live, cached, news))

    def attend(segments, state=None, last=False):
        arrays = []
        for array, *unused in segments:
            if not any(array is a for a in arrays):
                arrays.append(array)
        place = lambda array: [array is a for a in arrays].index(True)
        cuts = tuple((place(a), start, count, source) for a, start, count, source in segments)
        keys = sum(s[2] for s in segments)
        return call(
            functools.partial(attend_kernel, cuts, state is not None, last),
            final if last else [sds((rows * heads, HD), f32)] * 3,
            (rank, query, tags, own_order, live, *(state or ()), *arrays),
            1,
            flops=4 * rows * heads * HD * keys,
            moved=8 * rows * heads * keys,
        )

    def join(*cuts):
        out = sds((2, sum(c[2] for c in cuts), HD), bf16)
        return call(functools.partial(join_kernel, [c[1:] for c in cuts]), out, [c[0] for c in cuts])

    ctx = lambda x, k: swap(x, "ctx", n_ctx, k)
    old, new = cache.shape[1], rows
    c4 = ctx(cache, 4)
    c2 = ctx(cache, 2)
    c1 = ctx(cache, 1)
    c3 = ctx(c2, 1)
    c6 = ctx(c4, 2)
    f4 = ctx(fresh, 4)
    f2 = ctx(fresh, 2)
    f6 = ctx(f4, 2)
    ux = ctx(join((fresh, 0, new), (c6, 0, old)), 1)
    c5 = ctx(c4, 1)
    xa = ctx(join((f2, 0, new), (f4, 0, new)), 1)
    xb = ctx(f6, 1)
    state = attend([(c, 0, old, None) for c in (cache, c2, c4, c1)])
    state = attend(
        [(c3, 0, old, None), (c5, 0, old, None), (c6, 0, old, None), (ux, new, old, None)]
        + [(fresh, 0, new, 0), (ux, 0, new, 1), (f2, 0, new, 2), (f4, 0, new, 4), (f6, 0, new, 6)],
        state,
    )
    return attend([(xa, 0, new, 3), (xa, new, new, 5), (xb, 0, new, 7)], state, True)


def paired(n_ctx):
    return n_ctx == 8


def solution(mesh):
    in_specs = (
        P("ctx", "tp"),
        P(),
        P(None, "tp"),
        P("tp"),
        P(None, "tp"),
        P("tp"),
        P(None, "tp"),
        P("tp"),
        P("ctx", "tp"),
        P("ctx", "tp"),
        P(),
        P(),
    )

    return jax.shard_map(local, mesh=mesh, in_specs=in_specs, out_specs=P("ctx", "tp"), check_vma=False)
```

```python
import functools

import jax
import jax.numpy as jnp
from jax import lax
from jax.experimental import pallas as pl
from jax.experimental.pallas import tpu as pltpu
from jax.sharding import PartitionSpec as P


HD = 128
LOG2E = 1.4426950408889634

EARLY = 4


def swap(x, axis, n, k):
    return lax.ppermute(x, axis, [(i, i ^ k) for i in range(n)])


def flip(row):
    n = row.shape[1]
    eye = lax.broadcasted_iota(jnp.int32, (n, n), 0) == lax.broadcasted_iota(jnp.int32, (n, n), 1)
    return jnp.sum(jnp.where(eye, row, jnp.zeros_like(row)), axis=1, keepdims=True)


def start_copies(pairs, sems):
    copies = [pltpu.make_async_copy(a, b, sems.at[i]) for i, (a, b) in enumerate(pairs)]
    for copy in copies:
        copy.start()
    return copies


def stack_kernel(key_in, value_in, stacked, sems):
    for copy in start_copies([(key_in, stacked.at[0]), (value_in, stacked.at[1])], sems):
        copy.wait()


def part_of(weight, me, j, parts):
    depth = weight.shape[0] // parts
    return weight.at[pl.ds(pl.multiple_of((me ^ j) * depth, depth), depth), :]


def setup_kernel(moved, parts, rank_ref, me_ref, keep_in, spots_in, w_query, *refs):
    sources, targets = refs[:moved], refs[moved : 2 * moved]
    weights, refs = refs[2 * moved : 2 * moved + EARLY], refs[2 * moved + EARLY :]
    cosine, sine, tags, order, live, keep, spots, sems = refs
    rank = rank_ref[0]
    copies = start_copies(
        [(keep_in, keep), (spots_in, spots)]
        + list(zip(sources, targets))
        + [(part_of(w_query, me_ref[0], j, parts), weight) for j, weight in enumerate(weights)],
        sems,
    )
    copies[0].wait()
    copies[1].wait()
    blocks, rows = keep.shape
    kept = keep[...].astype(jnp.float32)
    upper = lax.broadcasted_iota(jnp.int32, (rows, rows), 0) < lax.broadcasted_iota(jnp.int32, (rows, rows), 1)
    inner = jnp.dot(kept.astype(jnp.bfloat16), upper.astype(jnp.bfloat16), preferred_element_type=jnp.float32)
    counts = jnp.broadcast_to(jnp.sum(kept, axis=1, keepdims=True), (blocks, rows))
    lower = lax.broadcasted_iota(jnp.int32, (blocks, blocks), 1) < lax.broadcasted_iota(jnp.int32, (blocks, blocks), 0)
    before = jnp.dot(lower.astype(jnp.bfloat16), counts.astype(jnp.bfloat16), preferred_element_type=jnp.float32)
    ordinals = inner + before
    tags[...] = jnp.where(kept > 0, ordinals, jnp.float32(2**30))
    mine = lax.broadcasted_iota(jnp.int32, (blocks, rows), 0) == rank
    order[...] = flip(jnp.sum(jnp.where(mine, ordinals, 0.0), axis=0, keepdims=True))
    live[...] = flip(jnp.sum(jnp.where(mine, kept, 0.0), axis=0, keepdims=True))

    where = spots[:, pl.ds(pl.multiple_of(rank * rows, rows), rows)].astype(jnp.float32)
    half = HD // 2
    freq = lax.rem(lax.broadcasted_iota(jnp.int32, (1, HD), 1), half)
    inv = jnp.exp(-(2.0 * freq.astype(jnp.float32) / HD) * jnp.log(jnp.full((1, 1), 1000000.0, jnp.float32)))
    picked = jnp.where(
        freq < HD // 8,
        flip(where[0:1]),
        jnp.where(freq < HD // 8 + 3 * HD // 16, flip(where[1:2]), flip(where[2:3])),
    )
    angle = picked * inv
    cosine[...] = jnp.cos(angle)
    low = lax.broadcasted_iota(jnp.int32, (1, HD), 1) < half
    sine[...] = jnp.where(low, -1.0, 1.0) * jnp.sin(angle)
    for copy in copies[2:]:
        copy.wait()


def turn(x, cosine, sine):
    return x * cosine + pltpu.roll(x, HD // 2, 1) * sine


def wide(ref, start, count):
    block = ref[pl.ds(start, count), :]
    return jnp.concatenate([block[i : i + 1] for i in range(count)], axis=1)


def stack_rows_kernel(first, second, out):
    rows = first.shape[0]
    out[:rows, :] = first[...]
    out[rows:, :] = second[...]


def key_value_kernel(parts, *refs):
    me_ref = refs[0]
    gain, w_key, bias_key, w_value, bias_value, cosine, sine, normed, fresh = refs[3:]
    rows = normed.shape[0]
    hidden_refs = [ref.at[spot : spot + rows, :] for spot in (0, rows) for ref in refs[1:3]]
    width = normed.shape[1] // parts
    me = me_ref[0]
    square = None
    for ref in hidden_refs:
        x = ref[...].astype(jnp.float32)
        part = jnp.sum(x * x, axis=1, keepdims=True)
        square = part if square is None else square + part
    scale = lax.rsqrt(square * (1.0 / (width * parts)) + 1e-06)
    key_sum = value_sum = None
    for j, ref in enumerate(hidden_refs):
        spot = pl.multiple_of((me ^ j) * width, width)
        x = ref[...].astype(jnp.float32)
        piece = (x * scale * wide(gain, (me ^ j) * (width // HD), width // HD)).astype(jnp.bfloat16)
        normed[:, j * width : (j + 1) * width] = piece
        k = jnp.dot(piece, w_key[pl.ds(spot, width), :], preferred_element_type=jnp.float32)
        v = jnp.dot(piece, w_value[pl.ds(spot, width), :], preferred_element_type=jnp.float32)
        key_sum = k if key_sum is None else key_sum + k
        value_sum = v if value_sum is None else value_sum + v
    for h in range(key_sum.shape[1] // HD):
        cut = slice(h * HD, (h + 1) * HD)
        fresh[0, :, cut] = turn(key_sum[:, cut] + bias_key[h : h + 1, :], cosine[...], sine[...]).astype(jnp.bfloat16)
        fresh[1, :, cut] = (value_sum[:, cut] + bias_value[h : h + 1, :]).astype(jnp.bfloat16)


def query_kernel(parts, me_ref, normed, bias_query, cosine, sine, w_query, *refs):
    early, query = refs[:EARLY], refs[EARLY]
    width = normed.shape[1] // parts
    late = range(EARLY, parts)
    if late:
        weights, sems = refs[EARLY + 1 :]
        copies = start_copies([(part_of(w_query, me_ref[0], j, parts), weights.at[j - EARLY]) for j in late], sems)
    total = None
    for j in range(parts):
        if j >= EARLY:
            copies[j - EARLY].wait()
        weight = early[j][...] if j < EARLY else weights[j - EARLY]
        q = jnp.dot(normed[:, j * width : (j + 1) * width], weight, preferred_element_type=jnp.float32)
        total = q if total is None else total + q
    rows = normed.shape[0]
    for h in range(total.shape[1] // HD):
        cut = slice(h * HD, (h + 1) * HD)
        query[h * rows : (h + 1) * rows, :] = turn(
            total[:, cut] + bias_query[h : h + 1, :], cosine[...], sine[...]
        ).astype(jnp.bfloat16)


SCALE = LOG2E / (HD**0.5)


def fold(x):
    out = x[:, :HD]
    for spot in range(HD, x.shape[1], HD):
        out = out + x[:, spot : spot + HD]
    return out


def absorb(state, query, key, value, bias):
    rows, count = query.shape[0], key.shape[0]
    score = lax.dot_general(query, key, (((1,), (1,)), ((), ())), preferred_element_type=jnp.float32)
    if bias is not None:
        own = bias.shape[0]
        score = jnp.concatenate([score[r : r + own] + bias for r in range(0, rows, own)], axis=0)
    higher = jnp.broadcast_to(jnp.max(score, axis=1, keepdims=True), (rows, HD))
    if state is not None:
        peak, total, summed = state
        higher = jnp.maximum(peak, higher)
    weights = jnp.exp2((score - jnp.concatenate([higher] * (count // HD), axis=1)) * SCALE)
    sums = fold(weights)
    added = jnp.dot(weights.astype(jnp.bfloat16), value, preferred_element_type=jnp.float32)
    if state is None:
        return higher, sums, added
    shrink = jnp.exp2((peak - higher) * SCALE)
    return higher, total * shrink + sums, summed * shrink + added


def groups(segments):
    group, count = [], 0
    for segment in segments:
        group.append(segment)
        count += segment[2]
        if count >= (CHUNK if segment[3] is None else FRESH) or segment is segments[-1]:
            yield group
            group, count = [], 0


def attend_kernel(segments, given, last, *refs):
    refs = list(refs)
    rank, query, tags, order, live = refs[0][0], *refs[1:5]
    del refs[:5]
    state = None
    if given:
        state = tuple(ref[...] for ref in refs[:3])
        del refs[:3]
    q = query[...]
    for fresh in (False, True):
        for group in groups([s for s in segments if (s[3] is not None) == fresh]):
            key, value = [
                jnp.concatenate([refs[i][kind, start : start + count] for i, start, count, unused in group], axis=0)
                for kind in range(2)
            ]
            bias = None
            if fresh:
                tag = jnp.concatenate([tags[pl.ds(rank ^ s[3], 1), :] for s in group], axis=1)
                bias = jnp.where(tag <= order[...], 0.0, -jnp.inf)
            state = absorb(state, q, key, value, bias)
    finish(refs[len({s[0] for s in segments}) :], state, live, last)


def join_kernel(cuts, *refs):
    spot = 0
    for ref, (start, count) in zip(refs, cuts):
        refs[-1][:, spot : spot + count] = ref[:, start : start + count]
        spot += count


def finish(refs, state, live, last):
    if not last:
        for ref, part in zip(refs, state):
            ref[...] = part
        return
    out = refs[0]
    count = out.shape[0]
    result = state[2] * (1.0 / jnp.sum(state[1], axis=1, keepdims=True))
    for h in range(result.shape[0] // count):
        out[:, h * HD : (h + 1) * HD] = (result[h * count : (h + 1) * count] * live[...]).astype(jnp.bfloat16)


def stacked_kernel(query, tags, order, live, cached, news, out):
    rows = query.shape[0]
    q = query[...]

    def plain(i, state):
        return absorb(state, q, cached[i, 0], cached[i, 1], None)

    def masked(i, state):
        bias = jnp.where(tags[pl.ds(i, 1), :] <= order[...], 0.0, -jnp.inf)
        return absorb(state, q, news[i, 0], news[i, 1], bias)

    state = (
        jnp.full((rows, HD), -1e30, jnp.float32),
        jnp.zeros((rows, HD), jnp.float32),
        jnp.zeros((rows, HD), jnp.float32),
    )
    state = lax.fori_loop(0, cached.shape[0], plain, state)
    state = lax.fori_loop(0, news.shape[0], masked, state)
    finish([out], state, live, True)


CHUNK = 512
FRESH = 384


def call(kernel, outs, args, scalars=0, far=(), scratch=(), flops=0, moved=0):
    many = isinstance(outs, (list, tuple))
    specs = [pl.BlockSpec(memory_space=pltpu.SMEM)] * scalars
    specs += [
        pl.BlockSpec(memory_space=pltpu.HBM if i in far else pltpu.VMEM) for i in range(scalars, len(args))
    ]
    out_specs = jax.tree.map(lambda _: pl.BlockSpec(memory_space=pltpu.VMEM), list(outs) if many else outs)
    args = [pltpu.with_memory_space_constraint(a, pltpu.HBM) if i in far else a for i, a in enumerate(args)]
    return pl.pallas_call(
        kernel,
        out_shape=list(outs) if many else outs,
        in_specs=specs,
        out_specs=out_specs,
        scratch_shapes=list(scratch),
        compiler_params=pltpu.CompilerParams(vmem_limit_bytes=20 * 1024 * 1024),
        cost_estimate=pl.CostEstimate(flops=flops, bytes_accessed=moved, transcendentals=0),
    )(*args)


def local(
    hidden,
    norm_gain,
    w_query,
    bias_query,
    w_key,
    bias_key,
    w_value,
    bias_value,
    cache_key,
    cache_value,
    keep,
    positions,
):
    n_ctx, n_tp = lax.axis_size("ctx"), lax.axis_size("tp")
    rank = lax.axis_index("ctx")[None].astype(jnp.int32)
    me = lax.axis_index("tp")[None].astype(jnp.int32)
    rows, width = hidden.shape
    kv_width = w_key.shape[1]
    heads = w_query.shape[1] // HD
    sds = jax.ShapeDtypeStruct
    f32, bf16 = jnp.float32, jnp.bfloat16

    far_hidden = swap(hidden, "tp", n_tp, 2)

    carried = (
        hidden,
        norm_gain.reshape(-1, HD),
        w_key,
        bias_key.reshape(-1, HD),
        w_value,
        bias_value.reshape(-1, HD),
        bias_query.reshape(-1, HD),
    )
    cache = call(
        stack_kernel,
        sds((2, *cache_key.shape), bf16),
        (cache_key, cache_value),
        far=(0, 1),
        scratch=[pltpu.SemaphoreType.DMA((2,))],
        moved=1000000,
    )
    setup = call(
        functools.partial(setup_kernel, len(carried), n_tp),
        [sds(a.shape, a.dtype) for a in carried]
        + [sds((width, heads * HD), bf16)] * EARLY
        + [
            sds((rows, HD), f32),
            sds((rows, HD), f32),
            sds((n_ctx, rows), f32),
            sds((rows, 1), f32),
            sds((rows, 1), f32),
        ],
        (rank, me, keep.reshape(n_ctx, rows), positions, w_query, *carried),
        2,
        range(2, 5 + len(carried)),
        [
            pltpu.VMEM((n_ctx, rows), jnp.int32),
            pltpu.VMEM(positions.shape, jnp.int32),
            pltpu.SemaphoreType.DMA((2 + EARLY + len(carried),)),
        ],
        0,
        4000000,
    )
    own_hidden, gain, key_weight, key_bias, value_weight, value_bias, query_bias = setup[:7]
    early = setup[7 : 7 + EARLY]
    cosine, sine, tags, own_order, live = setup[7 + EARLY :]

    halves = call(stack_rows_kernel, sds((2 * rows, width), bf16), (own_hidden, far_hidden))
    beside = swap(halves, "tp", n_tp, 1)
    normed, fresh = call(
        functools.partial(key_value_kernel, n_tp),
        (sds((rows, width * n_tp), bf16), sds((2, rows, kv_width), bf16)),
        (me, halves, beside, gain, key_weight, key_bias, value_weight, value_bias, cosine, sine),
        1,
        flops=2 * rows * width * n_tp * 2 * kv_width,
        moved=3000000,
    )
    late = ()
    if n_tp > EARLY:
        late = (pltpu.VMEM((n_tp - EARLY, width, heads * HD), bf16), pltpu.SemaphoreType.DMA((n_tp - EARLY,)))
    query = call(
        functools.partial(query_kernel, n_tp),
        sds((rows * heads, HD), bf16),
        (me, normed, query_bias, cosine, sine, w_query, *early),
        1,
        (5,),
        late,
        flops=2 * rows * width * n_tp * heads * HD,
        moved=7000000,
    )
    final = sds((rows, heads * HD), bf16)
    if not paired(n_ctx):
        cached = lax.all_gather(cache, "ctx", axis=0)
        news = lax.all_gather(fresh, "ctx", axis=0)
        return call(stacked_kernel, final, (query, tags, own_order, live, cached, news))

    def attend(segments, state=None, last=False):
        arrays = []
        for array, *unused in segments:
            if not any(array is a for a in arrays):
                arrays.append(array)
        place = lambda array: [array is a for a in arrays].index(True)
        cuts = tuple((place(a), start, count, source) for a, start, count, source in segments)
        keys = sum(s[2] for s in segments)
        return call(
            functools.partial(attend_kernel, cuts, state is not None, last),
            final if last else [sds((rows * heads, HD), f32)] * 3,
            (rank, query, tags, own_order, live, *(state or ()), *arrays),
            1,
            flops=4 * rows * heads * HD * keys,
            moved=8 * rows * heads * keys,
        )

    def join(*cuts):
        out = sds((2, sum(c[2] for c in cuts), HD), bf16)
        return call(functools.partial(join_kernel, [c[1:] for c in cuts]), out, [c[0] for c in cuts])

    ctx = lambda x, k: swap(x, "ctx", n_ctx, k)
    old, new = cache.shape[1], rows
    c4 = ctx(cache, 4)
    c2 = ctx(cache, 2)
    c1 = ctx(cache, 1)
    c3 = ctx(c2, 1)
    c6 = ctx(c4, 2)
    f4 = ctx(fresh, 4)
    f2 = ctx(fresh, 2)
    f6 = ctx(f4, 2)
    ux = ctx(join((fresh, 0, new), (c6, 0, old)), 1)
    c5 = ctx(c4, 1)
    xa = ctx(join((f2, 0, new), (f4, 0, new)), 1)
    xb = ctx(f6, 1)
    state = attend([(c, 0, old, None) for c in (cache, c2, c4, c1)])
    state = attend(
        [(c3, 0, old, None), (c5, 0, old, None), (c6, 0, old, None), (ux, new, old, None)]
        + [(fresh, 0, new, 0), (ux, 0, new, 1), (f2, 0, new, 2), (f4, 0, new, 4), (f6, 0, new, 6)],
        state,
    )
    return attend([(xa, 0, new, 3), (xa, new, new, 5), (xb, 0, new, 7)], state, True)


def paired(n_ctx):
    return n_ctx == 8


def solution(mesh):
    in_specs = (
        P("ctx", "tp"),
        P(),
        P(None, "tp"),
        P("tp"),
        P(None, "tp"),
        P("tp"),
        P(None, "tp"),
        P("tp"),
        P("ctx", "tp"),
        P("ctx", "tp"),
        P(),
        P(),
    )

    return jax.shard_map(local, mesh=mesh, in_specs=in_specs, out_specs=P("ctx", "tp"), check_vma=False)
```
